32 devices in a mesh: grp: 4 (over y, x), lon: 8 (over z, core).
Axes of the slice: x: 2, y: 2, z: 4, core: 2. Of those that a mesh axis runs over, the one named last changes fastest.
Arguments:
- surface_temp: float32 [256, 8192], P('grp', 'lon'), may hold values from -1.9 to 0.6
- salinity: float32 [256, 8192], P('grp', 'lon'), may hold values from 30 to 35
- wind_stress: float32 [2, 256, 8192], P(None, 'grp', 'lon'), may hold values from -6 to 6
- ocean_current: float32 [2, 256, 8192], P(None, 'grp', 'lon'), may hold values from -3 to 3
- velocity: float32 [2, 256, 8192], P(None, 'grp', 'lon'), may hold values from -3 to 3
- stress: float32 [3, 256, 8192], P(None, 'grp', 'lon'), may hold values from -3 to 3
- ice_area: float32 [1024, 5, 2048], P(('grp', 'lon')), may hold values from 0.13 to 0.2
- ice_volume: float32 [1024, 5, 2048], P(('grp', 'lon')), may hold values from 0.1 to 1.5
- air_temp: float32 [1024, 2048], P(('grp', 'lon')), may hold values from -30 to -5
- ice_mask: int32 [1024], P(('grp', 'lon')), may hold values 0 or 1
- curve_pos: int32 [1024], P(('grp', 'lon')), may hold values from 0 to 255, as said below
Outputs:
- velocity_out: float32 [2, 256, 8192], P(None, 'grp', 'lon')
- stress_out: float32 [3, 256, 8192], P(None, 'grp', 'lon')
- area_out: float32 [1024, 5, 2048], P(('grp', 'lon'))
- volume_out: float32 [1024, 5, 2048], P(('grp', 'lon'))
The draws below stay inside these ranges and needn't reach their ends.
Inputs may be any that keep to these rules, and one draw needn't show every extreme that they name: `curve_pos`: each band's curve holds each position once; ice device j of a band holds positions j * 32 to (j + 1) * 32 - 1; from one tile to one ice device go at most 8 blocks, and exactly 8 for some pairs.
All inputs are finite; a program needn't handle non-finite values. No bound on the sum of `ice_mask` on one device may be relied on, other than what follows from the above.
Results may differ from the reference program's by a relative error of at most 0.000025.
Values sent between devices are 32-bit elements; how exact they have to be, the bound alone decides.
A program may use at most 64 MiB of HBM per device.

```python
import math
import jax
import jax.numpy as jnp
from jax import lax

NCAT = 5
BY = 8
BX = 256
BLX = 4
BLY = 8
SUB = 4
BLK = 32
NY = 256
NX = 8192
NBLK = 1024
N_GRP = 4
N_LON = 8


def routing(base_key):
    half_cap = BLK // N_LON

    def band_of(band_key):
        key_pairs, key_shift, key_tiles, key_seats = jax.random.split(band_key, 4)
        pairs = jax.random.permutation(key_pairs, N_LON)
        shifts = jax.random.randint(key_shift, (N_LON // 2,), 0, half_cap + 1).at[0].set(half_cap)
        counts = jnp.zeros((N_LON,), jnp.int32).at[pairs[0::2]].set(half_cap + shifts).at[pairs[1::2]].set(half_cap - shifts)
        ends = jnp.cumsum(counts)
        listed = jnp.arange(BLK, dtype=jnp.int32)
        offsets = jnp.sum((listed[:, None] >= ends[None, :]).astype(jnp.int32), axis=1)
        tiles = jnp.arange(N_LON, dtype=jnp.int32)
        targets = (tiles[:, None] + offsets[None, :]) % N_LON
        shuffles = jax.vmap(lambda one_key: jax.random.permutation(one_key, BLK))(jax.random.split(key_tiles, N_LON))
        seats = jax.vmap(lambda one_key: jax.random.permutation(one_key, BLK))(jax.random.split(key_seats, N_LON))
        positions = targets * BLK + seats[targets, listed[None, :]]
        curve = jnp.zeros((N_LON, BLK), jnp.int32).at[tiles[:, None], shuffles].set(positions)
        return curve.reshape(-1)
    curves = jax.vmap(band_of)(jax.random.split(base_key, N_GRP))
    return curves.reshape(-1)


def draw_curve_pos(key, part):
    return routing(jax.random.fold_in(key, 11))


def place_ends(entries, rng, low, high):
    longest = entries.shape.index(max(entries.shape))
    spots = []
    for shift in (0, 1):
        where = [jax.random.randint(jax.random.fold_in(rng, axis), (), 0, length) for axis, length in enumerate(entries.shape)]
        where[longest] = (where[longest] + shift) % entries.shape[longest]
        spots.append(tuple(where))
    return entries.at[spots[0]].set(low).at[spots[1]].set(high)


def steps_of(rng, shape, shards, least, top_value):
    gain = 1.0
    for dim, blocks in shards:
        draws = jax.random.uniform(jax.random.fold_in(jax.random.fold_in(rng, 6), dim), (blocks,), jnp.float32, least / len(shards), top_value / len(shards))
        gain = gain * jnp.repeat(jnp.exp(draws), shape[dim] // blocks).reshape((-1,) + (1,) * (len(shape) - 1 - dim))
    return gain


def centred(stream_key, extent, spread, bound, shards=(), held_as=jnp.bfloat16):
    loudness = steps_of(stream_key, extent, shards, -0.22, 0.18) if shards else 1.0
    values = jax.random.normal(stream_key, extent, jnp.float32) * spread * loudness
    return jnp.minimum(jnp.maximum(values, -bound), bound).astype(held_as)


def setup_inputs(seed: int = 0) -> dict:
    key_list = jax.random.split(jax.random.key(seed), 12)
    surface_temp = jnp.clip(-1.9 + 2.5 * jax.random.uniform(key_list[0], (NY, NX), jnp.float32) ** steps_of(key_list[0], (NY, NX), ((0, 4), (1, 8)), -0.2, 0.2), -1.9, 0.6)
    salinity = jnp.clip(30.0 + 5.0 * jax.random.uniform(key_list[1], (NY, NX), jnp.float32) ** steps_of(key_list[1], (NY, NX), ((0, 4), (1, 8)), -0.2, 0.2), 30.0, 35.0)
    wind_stress = centred(key_list[2], (2, NY, NX), 1.0, 6.0, ((1, 4), (2, 8)), jnp.float32)
    ocean_current = centred(key_list[3], (2, NY, NX), 0.5, 3.0, ((1, 4), (2, 8)), jnp.float32)
    velocity = centred(key_list[4], (2, NY, NX), 0.5, 3.0, ((1, 4), (2, 8)), jnp.float32)
    stress = centred(key_list[5], (3, NY, NX), 0.5, 3.0, ((1, 4), (2, 8)), jnp.float32)
    ice_area = jnp.clip(0.13 + 0.07000001 * jax.random.uniform(key_list[6], (NBLK, NCAT, BY * BX), jnp.float32) ** steps_of(key_list[6], (NBLK, NCAT, BY * BX), ((0, 32),), -0.2, 0.2), 0.13, 0.2)
    ice_volume = jnp.clip(jnp.exp(math.log(1.5) - 2.7080502 * jax.random.uniform(key_list[7], (NBLK, NCAT, BY * BX), jnp.float32) ** steps_of(key_list[7], (NBLK, NCAT, BY * BX), ((0, 32),), -0.2, 0.2)), 0.1, 1.5)
    air_temp = jnp.clip(-30.0 + 25.0 * jax.random.uniform(key_list[8], (NBLK, BY * BX), jnp.float32) ** steps_of(key_list[8], (NBLK, BY * BX), ((0, 32),), -0.2, 0.2), -30.0, -5.0)
    ice_mask = place_ends((jax.random.randint(key_list[9], (NBLK,), 0, 4) < 3).astype(jnp.int32), jax.random.fold_in(key_list[9], 1), 0, 1)
    curve_pos = draw_curve_pos(jax.random.fold_in(key_list[11], 71), 0)
    return dict(surface_temp=surface_temp, salinity=salinity, wind_stress=wind_stress, ocean_current=ocean_current, velocity=velocity, stress=stress, ice_area=ice_area, ice_volume=ice_volume, air_temp=air_temp, ice_mask=ice_mask, curve_pos=curve_pos)


KAPPA = 0.02
MELT = 0.6
PSTAR = 10.0
CSTAR = 20.0
RELAX = 0.4
ECC2 = 4.0
DMIN2 = 0.01
DTE = 0.5
DRAG = 1.0
FCOR = 0.3

def to_blocks(field_grid):
    shaped = field_grid.reshape(N_GRP, BLY, BY, N_LON, BLX, BX).transpose(0, 3, 1, 4, 2, 5)
    return shaped.reshape(NBLK, BY * BX)

def from_blocks(block_rows):
    shaped = block_rows.reshape(N_GRP, N_LON, BLY, BLX, BY, BX).transpose(0, 2, 4, 1, 3, 5)
    return shaped.reshape(NY, NX)

def thermo(area, volume, air, temp_blocks, salt_blocks, ocean):
    freeze = -0.054 * salt_blocks
    excess = temp_blocks - freeze
    growth = KAPPA * area * (freeze - air)[:, None, :] / (volume + 0.1)
    vol_new = (volume + growth) * jnp.exp(-MELT * excess)[:, None, :]
    area_new = area * jnp.exp(-0.5 * MELT * excess)[:, None, :]
    keep = ocean[:, None, None]
    area_keep = jnp.where(keep, area_new, area)
    volume_keep = jnp.where(keep, vol_new, volume)
    conc_sum = lax.optimization_barrier(jnp.sum(area_new, axis=1))
    mass_sum = lax.optimization_barrier(jnp.sum(vol_new, axis=1))
    conc = jnp.where(ocean[:, None], conc_sum, jnp.zeros_like(conc_sum))
    mass = jnp.where(ocean[:, None], mass_sum, jnp.zeros_like(mass_sum))
    strength = PSTAR * mass * jnp.exp(-CSTAR * (1.0 - conc))
    return (area_keep, volume_keep, jnp.stack([mass, strength], axis=1))

def extend(fields, signs, which):
    top_row = signs[:, None, None] * fields[:, -1:, ::-1]
    bottom_row = jnp.zeros_like(fields[:, :1])
    tall = jnp.concatenate([bottom_row, fields, top_row], axis=1)
    return jnp.concatenate([tall[:, :, -1:], tall, tall[:, :, :1]], axis=2)

def across(padded):
    return (padded[1:-1, 2:] - padded[1:-1, :-2]) * 0.5

def upward(padded):
    return (padded[2:, 1:-1] - padded[:-2, 1:-1]) * 0.5

def subcycle(velocity, stress, mass, strength, wind_stress, ocean_current, extend_fn):
    speed = extend_fn(velocity, jnp.array([-1.0, -1.0], jnp.float32), 'speed')
    dudx = across(speed[0])
    dudy = upward(speed[0])
    dvdx = across(speed[1])
    dvdy = upward(speed[1])
    divu = dudx + dvdy
    tension = dudx - dvdy
    shear = dudy + dvdx
    delta = jnp.sqrt(divu * divu + (tension * tension + shear * shear) / ECC2 + DMIN2)
    ratio = strength / delta
    sig_one = (stress[0] + RELAX * (ratio * divu - strength)) / (1.0 + RELAX)
    sig_two = (stress[1] + RELAX * ratio * tension / ECC2) / (1.0 + RELAX)
    sig_shear = (stress[2] + RELAX * ratio * shear / (2.0 * ECC2)) / (1.0 + RELAX)
    new_stress = jnp.stack([sig_one, sig_two, sig_shear])
    padded = extend_fn(new_stress, jnp.array([1.0, 1.0, 1.0], jnp.float32), 'stress')
    normal_x = (padded[0] + padded[1]) * 0.5
    normal_y = (padded[0] - padded[1]) * 0.5
    force_x = across(normal_x) + upward(padded[2])
    force_y = across(padded[2]) + upward(normal_y)
    inertia = mass / DTE
    denom = inertia + DRAG
    u_old = velocity[0]
    v_old = velocity[1]
    u_new = (inertia * u_old + force_x + wind_stress[0] + DRAG * ocean_current[0] + FCOR * mass * v_old) / denom
    v_new = (inertia * v_old + force_y + wind_stress[1] + DRAG * ocean_current[1] - FCOR * mass * u_old) / denom
    return (jnp.stack([u_new, v_new]), new_stress)

def reference(surface_temp, salinity, wind_stress, ocean_current, velocity, stress, ice_area, ice_volume, air_temp, ice_mask, curve_pos):
    band_start = jnp.arange(NBLK, dtype=jnp.int32) // (N_LON * BLK) * (N_LON * BLK)
    ice_index = (band_start + curve_pos).astype(jnp.int32)
    temp_ice = jnp.zeros((NBLK, BY * BX), jnp.float32).at[ice_index].set(to_blocks(surface_temp))
    salt_ice = jnp.zeros((NBLK, BY * BX), jnp.float32).at[ice_index].set(to_blocks(salinity))
    area_out, volume_out, coupled = thermo(ice_area, ice_volume, air_temp, temp_ice, salt_ice, ice_mask > 0)
    coupled_tile = coupled[ice_index]
    mass = from_blocks(coupled_tile[:, 0])
    strength = from_blocks(coupled_tile[:, 1])
    speed_now = velocity
    stress_now = stress
    for substep in range(SUB):
        speed_now, stress_now = subcycle(speed_now, stress_now, mass, strength, wind_stress, ocean_current, extend)
    return (speed_now, stress_now, area_out, volume_out)
```

```python
import functools

import jax
import jax.numpy as jnp
from jax import lax
from jax.experimental import pallas as pl
from jax.experimental.pallas import tpu as pltpu
from jax.sharding import PartitionSpec as P

BY = 8
BX = 256
SUB = 4

KAPPA = 0.02
MELT = 0.6
PSTAR = 10.0
CSTAR = 20.0
RELAX = 0.4
FCOR = 0.3

HALO = 2 * SUB
PAD = 8
LANES = 128
MESH = pl.DeviceIdType.MESH

N_FIELD = 9


def thermo(area, volume, air, temp_blocks, salt_blocks, ocean):
    freeze = -0.054 * salt_blocks
    excess = temp_blocks - freeze
    growth = KAPPA * area * (freeze - air)[:, None, :] / (volume + 0.1)
    vol_new = (volume + growth) * jnp.exp(-MELT * excess)[:, None, :]
    area_new = area * jnp.exp(-0.5 * MELT * excess)[:, None, :]
    keep = ocean[:, None, None]
    area_keep = jnp.where(keep, area_new, area)
    volume_keep = jnp.where(keep, vol_new, volume)
    conc_sum = jnp.sum(area_new, axis=1)
    mass_sum = jnp.sum(vol_new, axis=1)
    conc = jnp.where(ocean[:, None], conc_sum, jnp.zeros_like(conc_sum))
    mass = jnp.where(ocean[:, None], mass_sum, jnp.zeros_like(mass_sum))
    strength = PSTAR * mass * jnp.exp(-CSTAR * (1.0 - conc))
    return (area_keep, volume_keep, jnp.stack([mass, strength], axis=1))


def dynamics_kernel(
    n_grp, n_lon, vel_ref, str_ref, wind_ref, cur_ref, mass_ref, stg_ref, vel_out, str_out,
    ext, inv, mir, out_e, out_w, in_w, in_e, row_send, row_recv, col_send, col_recv,
):
    rows, cols = mass_ref.shape
    wide = cols + LANES
    top = PAD + HALO
    tall = rows + 2 * HALO
    g = lax.axis_index("grp")
    l = lax.axis_index("lon")
    east = lax.rem(l + 1, n_lon)
    west = lax.rem(l + n_lon - 1, n_lon)
    mirror = n_lon - 1 - l
    not_south = g > 0
    not_north = g < n_grp - 1
    north_g = jnp.where(not_north, g + 1, g)
    north_l = jnp.where(not_north, l, mirror)

    barrier = pltpu.get_barrier_semaphore()
    pl.semaphore_signal(barrier, inc=1, device_id={"grp": g, "lon": east}, device_id_type=MESH)
    pl.semaphore_signal(barrier, inc=1, device_id={"grp": g, "lon": west}, device_id_type=MESH)
    pl.semaphore_signal(
        barrier, inc=1, device_id={"grp": north_g, "lon": north_l}, device_id_type=MESH
    )

    @pl.when(not_south)
    def _():
        pl.semaphore_signal(
            barrier, inc=1, device_id={"grp": g - 1, "lon": l}, device_id_type=MESH
        )

    body = pl.ds(top, rows)
    main = pl.ds(0, cols)
    for f in range(2):
        ext[f, body, main] = vel_ref[f]
        ext[5 + f, body, main] = wind_ref[f] + cur_ref[f]
    for f in range(3):
        ext[2 + f, body, main] = str_ref[f]
    ext[7, body, main] = mass_ref[...]
    ext[8, body, main] = stg_ref[...]
    for f in range(N_FIELD):
        ext[f, pl.ds(0, PAD), :] = jnp.zeros((PAD, wide), jnp.float32)
        ext[f, pl.ds(top + rows + HALO, PAD), :] = jnp.zeros((PAD, wide), jnp.float32)

    @pl.when(jnp.logical_not(not_south))
    def _():
        for f in range(N_FIELD):
            ext[f, pl.ds(PAD, HALO), main] = jnp.zeros((HALO, cols), jnp.float32)

    @pl.when(jnp.logical_not(not_north))
    def _():
        a = lax.broadcasted_iota(jnp.int32, (LANES, LANES), 0)
        b = lax.broadcasted_iota(jnp.int32, (LANES, LANES), 1)
        flip = (a + b == LANES - 1).astype(jnp.float32)
        for f in range(N_FIELD):
            sign = -1.0 if f in (0, 1, 5, 6) else 1.0
            for c in range(cols // LANES):
                x = ext[f, pl.ds(top + rows - HALO, HALO), pl.ds(c * LANES, LANES)]
                y = sign * jnp.dot(
                    x, flip, precision=lax.Precision.HIGHEST, preferred_element_type=jnp.float32
                )
                for r in range(HALO):
                    mir[f, pl.ds(HALO - 1 - r, 1), pl.ds(cols - (c + 1) * LANES, LANES)] = y[
                        r : r + 1
                    ]

    pl.semaphore_wait(barrier, jnp.where(not_south, 4, 3))

    low = ext.at[:, pl.ds(PAD, HALO), main]
    high = ext.at[:, pl.ds(top + rows, HALO), main]
    first = ext.at[:, pl.ds(top, HALO), main]
    last = ext.at[:, pl.ds(top + rows - HALO, HALO), main]
    to_south = pltpu.make_async_remote_copy(
        src_ref=first, dst_ref=high, send_sem=row_send.at[0], recv_sem=row_recv.at[0],
        device_id={"grp": jnp.where(not_south, g - 1, g), "lon": l}, device_id_type=MESH,
    )
    to_north = pltpu.make_async_remote_copy(
        src_ref=last, dst_ref=low, send_sem=row_send.at[1], recv_sem=row_recv.at[1],
        device_id={"grp": north_g, "lon": l}, device_id_type=MESH,
    )
    to_mirror = pltpu.make_async_remote_copy(
        src_ref=mir, dst_ref=high, send_sem=row_send.at[1], recv_sem=row_recv.at[0],
        device_id={"grp": g, "lon": mirror}, device_id_type=MESH,
    )

    @pl.when(not_south)
    def _():
        to_south.start()

    @pl.when(not_north)
    def _():
        to_north.start()

    @pl.when(jnp.logical_not(not_north))
    def _():
        to_mirror.start()

    to_south.wait_recv()

    @pl.when(not_south)
    def _():
        to_north.wait_recv()

    lane = lax.broadcasted_iota(jnp.int32, (tall, LANES), 1)
    span = pl.ds(PAD, tall)
    east_pack = jnp.zeros((tall, LANES), jnp.float32)
    west_pack = jnp.zeros((tall, LANES), jnp.float32)
    for f in range(N_FIELD):
        here = (lane >= f * HALO) & (lane < (f + 1) * HALO)
        tail = ext[f, span, pl.ds(cols - LANES, LANES)]
        head = ext[f, span, pl.ds(0, LANES)]
        east_pack = jnp.where(here, pltpu.roll(tail, ((f + 1) * HALO) % LANES, 1), east_pack)
        west_pack = jnp.where(here, pltpu.roll(head, f * HALO, 1) if f else head, west_pack)
    out_e[...] = east_pack
    out_w[...] = west_pack
    to_east = pltpu.make_async_remote_copy(
        src_ref=out_e, dst_ref=in_w, send_sem=col_send.at[0], recv_sem=col_recv.at[0],
        device_id={"grp": g, "lon": east}, device_id_type=MESH,
    )
    to_west = pltpu.make_async_remote_copy(
        src_ref=out_w, dst_ref=in_e, send_sem=col_send.at[1], recv_sem=col_recv.at[1],
        device_id={"grp": g, "lon": west}, device_id_type=MESH,
    )
    to_east.start()
    to_west.start()
    to_east.wait_recv()
    to_west.wait_recv()
    from_west = in_w[...]
    from_east = in_e[...]
    for f in range(N_FIELD):
        e = pltpu.roll(from_east, LANES - f * HALO, 1) if f else from_east
        w = pltpu.roll(from_west, LANES - (f + 1) * HALO, 1)
        ext[f, span, pl.ds(cols, LANES)] = jnp.where(
            lane < HALO, e, jnp.where(lane >= LANES - HALO, w, 0.0)
        )

    inv[...] = 1.0 / (2.0 * ext[7, span, :] + 1.0)

    @pl.when(jnp.logical_not(not_south))
    def _():
        inv[pl.ds(0, HALO), :] = jnp.zeros((HALO, wide), jnp.float32)

    @pl.when(not_south)
    def _():
        to_south.wait_send()

    @pl.when(not_north)
    def _():
        to_north.wait_send()

    @pl.when(jnp.logical_not(not_north))
    def _():
        to_mirror.wait_send()

    to_east.wait_send()
    to_west.wait_send()

    def across(x):
        return pltpu.roll(x, wide - 1, 1) - pltpu.roll(x, 1, 1)

    sub = lax.broadcasted_iota(jnp.int32, (8, wide), 0)
    is_first = sub == 0
    is_last = sub == 7

    def three(f, r):
        return (
            ext[f, pl.ds(pl.multiple_of(r - 8, 8), 8), :],
            ext[f, pl.ds(r, 8), :],
            ext[f, pl.ds(pl.multiple_of(r + 8, 8), 8), :],
        )

    def upward(strips):
        below, here, above = strips
        return pltpu.roll(jnp.where(is_first, above, here), 7, 0) - pltpu.roll(
            jnp.where(is_last, below, here), 1, 0
        )

    scale = 1.0 / (1.0 + RELAX)

    def stress_strip(i, carry):
        r = pl.multiple_of(PAD + i * 8, 8)
        at = pl.ds(r, 8)
        u = three(0, r)
        v = three(1, r)
        u_y, v_y, u_x, v_x = upward(u), upward(v), across(u[1]), across(v[1])
        divu = (u_x + v_y) * 0.5
        tension = (u_x - v_y) * 0.5
        shear = (u_y + v_x) * 0.5
        square = divu * divu + (tension * tension + shear * shear) * 0.25 + 0.01
        strength = ext[8, at, :]
        ratio = strength * lax.rsqrt(square)
        ext[2, at, :] = (ext[2, at, :] + RELAX * (ratio * divu - strength)) * scale
        ratio = ratio * scale
        ext[3, at, :] = ext[3, at, :] * scale + (RELAX / 4.0) * (ratio * tension)
        ext[4, at, :] = ext[4, at, :] * scale + (RELAX / 8.0) * (ratio * shear)
        return carry

    def speed_strip(i, carry):
        r = pl.multiple_of(PAD + i * 8, 8)
        at = pl.ds(r, 8)
        one = three(2, r)
        two = three(3, r)
        mixed = three(4, r)
        s_x = across(one[1] + two[1])
        s_y = upward([x - y for x, y in zip(one, two)])
        c_x = across(mixed[1])
        c_y = upward(mixed)
        force_x = s_x * 0.25 + c_y * 0.5
        force_y = c_x * 0.5 + s_y * 0.25
        mass = ext[7, at, :]
        factor = inv[pl.ds(pl.multiple_of(i * 8, 8), 8), :]
        u = ext[0, at, :]
        v = ext[1, at, :]
        turn = FCOR * mass
        inertia = 2.0 * mass
        ext[0, at, :] = (inertia * u + force_x + ext[5, at, :] + turn * v) * factor
        ext[1, at, :] = (inertia * v + force_y + ext[6, at, :] - turn * u) * factor
        return carry

    def step(k, carry):
        lax.fori_loop(0, tall // 8, stress_strip, 0)
        lax.fori_loop(0, tall // 8, speed_strip, 0)
        return carry

    lax.fori_loop(0, SUB, step, 0)

    for f in range(2):
        vel_out[f] = ext[f, body, main]
    for f in range(3):
        str_out[f] = ext[2 + f, body, main]


def dynamics(velocity, stress, wind_stress, ocean_current, mass, strength):
    n_grp = lax.axis_size("grp")
    n_lon = lax.axis_size("lon")
    rows, cols = mass.shape
    wide = cols + LANES
    tall = rows + 2 * HALO
    edge = pltpu.VMEM((tall, LANES), jnp.float32)
    vmem = pl.BlockSpec(memory_space=pltpu.VMEM)
    return pl.pallas_call(
        functools.partial(dynamics_kernel, n_grp, n_lon),
        out_shape=(
            jax.ShapeDtypeStruct(velocity.shape, jnp.float32),
            jax.ShapeDtypeStruct(stress.shape, jnp.float32),
        ),
        in_specs=[vmem] * 6,
        out_specs=(vmem, vmem),
        scratch_shapes=[
            pltpu.VMEM((N_FIELD, tall + 2 * PAD, wide), jnp.float32),
            pltpu.VMEM((tall, wide), jnp.float32),
            pltpu.VMEM((N_FIELD, HALO, cols), jnp.float32),
            edge, edge, edge, edge,
            pltpu.SemaphoreType.DMA((2,)),
            pltpu.SemaphoreType.DMA((2,)),
            pltpu.SemaphoreType.DMA((2,)),
            pltpu.SemaphoreType.DMA((2,)),
        ],
        compiler_params=pltpu.CompilerParams(
            collective_id=1, has_side_effects=True, vmem_limit_bytes=32 << 20
        ),
        name="dynamics",
    )(velocity, stress, wind_stress, ocean_current, mass, strength)


def shards(
    surface_temp, salinity, wind_stress, ocean_current, velocity, stress,
    ice_area, ice_volume, air_temp, ice_mask, curve_pos,
):
    lon_count = lax.axis_size("lon")
    tile_rows, tile_cols = surface_temp.shape
    block_count = curve_pos.shape[0]
    capacity = 2 * block_count // lon_count
    cells = BY * BX
    slot_count = lon_count * capacity

    def pack(field_grid):
        shaped = field_grid.reshape(tile_rows // BY, BY, tile_cols // BX, BX).transpose(0, 2, 1, 3)
        return shaped.reshape(block_count, cells)

    def unpack(block_rows):
        shaped = block_rows.reshape(tile_rows // BY, tile_cols // BX, BY, BX).transpose(0, 2, 1, 3)
        return shaped.reshape(tile_rows, tile_cols)

    targets = curve_pos // block_count
    indices = jnp.arange(block_count, dtype=jnp.int32)
    ranking = jnp.sum(
        ((targets[:, None] == targets[None, :]) & (indices[None, :] < indices[:, None])).astype(
            jnp.int32
        ),
        axis=1,
    )
    send_slot = targets * capacity + ranking
    slot_ids = jnp.arange(slot_count, dtype=jnp.int32)
    hit = send_slot[None, :] == slot_ids[:, None]
    block_of_slot = jnp.sum(jnp.where(hit, indices[None, :], 0), axis=1)
    pos_slots = jnp.sum(jnp.where(hit, curve_pos[None, :] + 1, 0), axis=1).astype(jnp.float32) - 1.0
    ocean = ice_mask > 0
    payload = jnp.stack([pack(surface_temp), pack(salinity)], axis=1)
    outgoing = payload[block_of_slot]
    incoming, in_pos = (
        lax.all_to_all(outgoing, "lon", split_axis=0, concat_axis=0, tiled=True),
        lax.all_to_all(pos_slots, "lon", split_axis=0, concat_axis=0, tiled=True),
    )
    local = in_pos.astype(jnp.int32) - lax.axis_index("lon") * block_count
    local = jnp.where(in_pos >= 0.0, local, block_count)
    arrive_slot = jnp.sum(
        jnp.where(local[None, :] == indices[:, None], slot_ids[None, :], 0), axis=1
    )
    arrived = incoming[arrive_slot]
    area_out, volume_out, coupled = thermo(
        ice_area, ice_volume, air_temp, arrived[:, 0], arrived[:, 1], ocean
    )
    replies = coupled[jnp.minimum(local, block_count - 1)]
    returned = lax.all_to_all(replies, "lon", split_axis=0, concat_axis=0, tiled=True)
    coupled_tile = returned[send_slot]
    mass = unpack(coupled_tile[:, 0])
    strength = unpack(coupled_tile[:, 1])
    velocity_out, stress_out = dynamics(
        velocity, stress, wind_stress, ocean_current, mass, strength
    )
    return (velocity_out, stress_out, area_out, volume_out)


def solution(mesh):
    return jax.shard_map(
        shards,
        mesh=mesh,
        in_specs=(
            P("grp", "lon"),
            P("grp", "lon"),
            P(None, "grp", "lon"),
            P(None, "grp", "lon"),
            P(None, "grp", "lon"),
            P(None, "grp", "lon"),
            P(("grp", "lon"), None, None),
            P(("grp", "lon"), None, None),
            P(("grp", "lon"), None),
            P(("grp", "lon")),
            P(("grp", "lon")),
        ),
        out_specs=(
            P(None, "grp", "lon"),
            P(None, "grp", "lon"),
            P(("grp", "lon"), None, None),
            P(("grp", "lon"), None, None),
        ),
        check_vma=False,
    )
```

```python
import functools

import jax
import jax.numpy as jnp
from jax import lax
from jax.experimental import pallas as pl
from jax.experimental.pallas import tpu as pltpu
from jax.sharding import PartitionSpec as P

BY = 8
BX = 256
SUB = 4

KAPPA = 0.02
MELT = 0.6
PSTAR = 10.0
CSTAR = 20.0
RELAX = 0.4
FCOR = 0.3

HALO = 2 * SUB
PAD = 8
LANES = 128
MESH = pl.DeviceIdType.MESH

N_FIELD = 9


def thermo(area, volume, air, temp_blocks, salt_blocks, ocean):
    freeze = -0.054 * salt_blocks
    excess = temp_blocks - freeze
    growth = KAPPA * area * (freeze - air)[:, None, :] / (volume + 0.1)
    vol_new = (volume + growth) * jnp.exp(-MELT * excess)[:, None, :]
    area_new = area * jnp.exp(-0.5 * MELT * excess)[:, None, :]
    keep = ocean[:, None, None]
    area_keep = jnp.where(keep, area_new, area)
    volume_keep = jnp.where(keep, vol_new, volume)
    return (area_keep, volume_keep)


def exact_dot(a, b):
    return jnp.dot(a, b, precision=lax.Precision.HIGHEST, preferred_element_type=jnp.float32)


def coupled_kernel(
    n_grp, n_lon, pos_row_ref, pos_col_ref, keep_ref, temp_ref, salt_ref, wind_ref, cur_ref,
    vel_ref, str_ref, area_ref, volume_ref, air_ref, vel_out, str_out, arrived_out,
    ext, inv, mir, out_e, out_w, in_w, in_e,
    blocks, flat, sums, slot_sums, pos_send, pos_recv, sea_send, sea_recv, ice_send, ice_recv,
    row_send, row_recv, col_send, col_recv, a2a_send, a2a_recv,
):
    rows, cols = temp_ref.shape
    wide = cols + LANES
    top = PAD + HALO
    tall = rows + 2 * HALO
    n_block, cells = air_ref.shape
    cap = sea_send.shape[2]
    n_slot = n_lon * cap
    g = lax.axis_index("grp")
    l = lax.axis_index("lon")
    east = lax.rem(l + 1, n_lon)
    west = lax.rem(l + n_lon - 1, n_lon)
    mirror = n_lon - 1 - l
    not_south = g > 0
    not_north = g < n_grp - 1

    barrier = pltpu.get_barrier_semaphore()

    def peer(d):
        return lax.rem(l + d, n_lon)

    def source(d):
        return lax.rem(l + n_lon - d, n_lon)

    for d in range(1, n_lon):
        pl.semaphore_signal(
            barrier, inc=1, device_id={"grp": g, "lon": peer(d)}, device_id_type=MESH
        )

    @pl.when(not_south)
    def _():
        pl.semaphore_signal(
            barrier, inc=1, device_id={"grp": g - 1, "lon": l}, device_id_type=MESH
        )

    @pl.when(not_north)
    def _():
        pl.semaphore_signal(
            barrier, inc=1, device_id={"grp": g + 1, "lon": l}, device_id_type=MESH
        )

    near = sorted(range(1, n_lon), key=lambda d: (min(d, n_lon - d), d))
    far = near[::-1]

    pos_row = pos_row_ref[...]
    to_row = jnp.floor(pos_row * (1.0 / n_block))
    to_col = jnp.floor(pos_col_ref[...] * (1.0 / n_block))
    down = lax.broadcasted_iota(jnp.int32, (n_block, n_block), 0)
    along = lax.broadcasted_iota(jnp.int32, (n_block, n_block), 1)
    same = to_col == to_row
    rank_row = jnp.sum(jnp.where(same & (down < along), 1.0, 0.0), axis=0, keepdims=True)
    rank_col = jnp.sum(jnp.where(same & (along < down), 1.0, 0.0), axis=1, keepdims=True)
    slot_row = to_row * cap + rank_row
    slot_col = to_col * cap + rank_col
    slot_down = lax.broadcasted_iota(jnp.int32, (n_slot, n_block), 0).astype(jnp.float32)
    slot_along = lax.broadcasted_iota(jnp.int32, (n_block, n_slot), 1).astype(jnp.float32)
    to_slots = jnp.where(slot_down == slot_row, 1.0, 0.0)
    from_slots = jnp.where(slot_along == slot_col, 1.0, 0.0)
    pos_slot = jnp.sum(to_slots * (pos_row + 1.0), axis=1, keepdims=True) - 1.0
    pos_wide = jnp.broadcast_to(pos_slot, (n_slot, LANES))
    for p in range(n_lon):
        pos_send[p] = pos_wide[p * cap : (p + 1) * cap]

    for f, ref in enumerate((temp_ref, salt_ref)):
        for i in range(rows):
            for c in range(cols // BX):
                blocks[f, pl.ds((i // BY) * (cols // BX) + c, 1), pl.ds((i % BY) * BX, BX)] = ref[
                    pl.ds(i, 1), pl.ds(c * BX, BX)
                ]
    for f in range(2):
        packed = exact_dot(to_slots, blocks[f])
        for p in range(n_lon):
            sea_send[p, f] = packed[p * cap : (p + 1) * cap]

    pl.semaphore_wait(
        barrier, n_lon - 1 + jnp.where(not_south, 1, 0) + jnp.where(not_north, 1, 0)
    )

    def lon_copy(kind, src, dst, d):
        return pltpu.make_async_remote_copy(
            src_ref=src.at[peer(d)], dst_ref=dst.at[l],
            send_sem=a2a_send.at[kind, d], recv_sem=a2a_recv.at[kind, d],
            device_id={"grp": g, "lon": peer(d)}, device_id_type=MESH,
        )

    pos_copy = {d: lon_copy(0, pos_send, pos_recv, d) for d in near}
    sea_copy = {d: lon_copy(1, sea_send, sea_recv, d) for d in near}
    ice_copy = {d: lon_copy(2, ice_send, ice_recv, d) for d in near}
    for d in far:
        pos_copy[d].start()
    for d in far:
        sea_copy[d].start()
    pos_recv[l] = pos_send[l]
    sea_recv[l] = sea_send[l]

    body = pl.ds(top, rows)
    main = pl.ds(0, cols)
    for f in range(2):
        ext[f, body, main] = vel_ref[f]
        ext[5 + f, body, main] = wind_ref[f] + cur_ref[f]
    for f in range(3):
        ext[2 + f, body, main] = str_ref[f]
    for f in range(N_FIELD):
        ext[f, pl.ds(0, PAD), :] = jnp.zeros((PAD, wide), jnp.float32)
        ext[f, pl.ds(top + rows + HALO, PAD), :] = jnp.zeros((PAD, wide), jnp.float32)

    @pl.when(jnp.logical_not(not_south))
    def _():
        for f in range(N_FIELD):
            ext[f, pl.ds(PAD, HALO), main] = jnp.zeros((HALO, cols), jnp.float32)

    lane = lax.broadcasted_iota(jnp.int32, (tall, LANES), 1)
    span = pl.ds(PAD, tall)

    def row_start(part, lo, n):
        fs = pl.ds(lo, n)

        @pl.when(jnp.logical_not(not_north))
        def _():
            a = lax.broadcasted_iota(jnp.int32, (LANES, LANES), 0)
            b = lax.broadcasted_iota(jnp.int32, (LANES, LANES), 1)
            flip = (a + b == LANES - 1).astype(jnp.float32)
            for f in range(lo, lo + n):
                sign = -1.0 if f in (0, 1, 5, 6) else 1.0
                for c in range(cols // LANES):
                    x = ext[f, pl.ds(top + rows - HALO, HALO), pl.ds(c * LANES, LANES)]
                    y = sign * exact_dot(x, flip)
                    for r in range(HALO):
                        mir[f, pl.ds(HALO - 1 - r, 1), pl.ds(cols - (c + 1) * LANES, LANES)] = y[
                            r : r + 1
                        ]

        low = ext.at[fs, pl.ds(PAD, HALO), main]
        high = ext.at[fs, pl.ds(top + rows, HALO), main]
        to_south = pltpu.make_async_remote_copy(
            src_ref=ext.at[fs, pl.ds(top, HALO), main], dst_ref=high,
            send_sem=row_send.at[part, 0], recv_sem=row_recv.at[part, 0],
            device_id={"grp": jnp.where(not_south, g - 1, g), "lon": l}, device_id_type=MESH,
        )
        to_north = pltpu.make_async_remote_copy(
            src_ref=ext.at[fs, pl.ds(top + rows - HALO, HALO), main], dst_ref=low,
            send_sem=row_send.at[part, 1], recv_sem=row_recv.at[part, 1],
            device_id={"grp": jnp.where(not_north, g + 1, g), "lon": l}, device_id_type=MESH,
        )
        to_mirror = pltpu.make_async_remote_copy(
            src_ref=mir.at[fs], dst_ref=high,
            send_sem=row_send.at[part, 1], recv_sem=row_recv.at[part, 0],
            device_id={"grp": g, "lon": mirror}, device_id_type=MESH,
        )

        @pl.when(not_south)
        def _():
            to_south.start()

        @pl.when(not_north)
        def _():
            to_north.start()

        @pl.when(jnp.logical_not(not_north))
        def _():
            to_mirror.start()

        return to_south, to_north, to_mirror

    def row_finish(copies):
        to_south, to_north, to_mirror = copies
        to_south.wait_recv()

        @pl.when(not_south)
        def _():
            to_north.wait_recv()

        @pl.when(not_south)
        def _():
            to_south.wait_send()

        @pl.when(not_north)
        def _():
            to_north.wait_send()

        @pl.when(jnp.logical_not(not_north))
        def _():
            to_mirror.wait_send()

    def col_start(part, lo, n):
        east_pack = jnp.zeros((tall, LANES), jnp.float32)
        west_pack = jnp.zeros((tall, LANES), jnp.float32)
        for k in range(n):
            here = (lane >= k * HALO) & (lane < (k + 1) * HALO)
            tail = ext[lo + k, span, pl.ds(cols - LANES, LANES)]
            head = ext[lo + k, span, pl.ds(0, LANES)]
            east_pack = jnp.where(here, pltpu.roll(tail, (k + 1) * HALO, 1), east_pack)
            west_pack = jnp.where(here, pltpu.roll(head, k * HALO, 1) if k else head, west_pack)
        out_e[part] = east_pack
        out_w[part] = west_pack
        to_east = pltpu.make_async_remote_copy(
            src_ref=out_e.at[part], dst_ref=in_w.at[part],
            send_sem=col_send.at[part, 0], recv_sem=col_recv.at[part, 0],
            device_id={"grp": g, "lon": east}, device_id_type=MESH,
        )
        to_west = pltpu.make_async_remote_copy(
            src_ref=out_w.at[part], dst_ref=in_e.at[part],
            send_sem=col_send.at[part, 1], recv_sem=col_recv.at[part, 1],
            device_id={"grp": g, "lon": west}, device_id_type=MESH,
        )
        to_east.start()
        to_west.start()
        return to_east, to_west

    def col_finish(part, lo, n, copies):
        for copy in copies:
            copy.wait()
        from_west = in_w[part]
        from_east = in_e[part]
        for k in range(n):
            e = pltpu.roll(from_east, LANES - k * HALO, 1) if k else from_east
            w = pltpu.roll(from_west, LANES - (k + 1) * HALO, 1)
            ext[lo + k, span, pl.ds(cols, LANES)] = jnp.where(
                lane < HALO, e, jnp.where(lane >= LANES - HALO, w, 0.0)
            )

    early_rows = row_start(0, 0, 7)

    keep = keep_ref[...] > 0.0
    n_cat = area_ref.shape[0]
    chunk = 512

    def reduce_chunk(i, carry):
        at = pl.ds(pl.multiple_of(i * chunk, chunk), chunk)
        area_sum = jnp.zeros((n_block, chunk), jnp.float32)
        vol_sum = jnp.zeros((n_block, chunk), jnp.float32)
        rate = jnp.zeros((n_block, chunk), jnp.float32)
        for c in range(n_cat):
            area = area_ref[c, :, at]
            vol = volume_ref[c, :, at]
            area_sum = area_sum + area
            vol_sum = vol_sum + vol
            rate = rate + area / (vol + 0.1)
        rate = KAPPA * rate
        sums[0, :, at] = jnp.where(keep, area_sum, 0.0)
        sums[1, :, at] = jnp.where(keep, vol_sum - rate * air_ref[:, at], 0.0)
        sums[2, :, at] = jnp.where(keep, rate, 0.0)
        return carry

    lax.fori_loop(0, cells // chunk, reduce_chunk, 0)

    for d in near:
        pos_copy[d].wait_recv()
    base = (l * n_block).astype(jnp.float32)
    for p in range(n_lon):
        flat[pl.ds(p * cap, cap), pl.ds(0, LANES)] = pos_recv[p]
    local = flat[:, pl.ds(0, LANES)] - base
    block_along = lax.broadcasted_iota(jnp.int32, (n_slot, LANES), 1).astype(jnp.float32)
    at_slot = jnp.where((local == block_along) & (block_along < n_block), 1.0, 0.0)
    for f in range(3):
        gathered = exact_dot(at_slot[:, :n_block], sums[f])
        for p in range(n_lon):
            slot_sums[p, f] = gathered[p * cap : (p + 1) * cap]

    row_finish(early_rows)
    early_cols = col_start(0, 0, 7)

    def answer(p):
        freeze = -0.054 * sea_recv[p, 1]
        decay = jnp.exp((-0.5 * MELT) * (sea_recv[p, 0] - freeze))
        mass = (slot_sums[p, 1] + slot_sums[p, 2] * freeze) * (decay * decay)
        conc = slot_sums[p, 0] * decay
        return mass, PSTAR * mass * jnp.exp(-CSTAR * (1.0 - conc))

    own_mass, own_strength = answer(l)
    ice_recv[l, 0] = own_mass
    ice_recv[l, 1] = own_strength
    for d in near:
        sea_copy[d].wait_recv()
        mass, strength = answer(source(d))
        ice_send[source(d), 0] = mass
        ice_send[source(d), 1] = strength
        ice_copy[n_lon - d].start()

    col_finish(0, 0, 7, early_cols)

    for f in range(2):
        for p in range(n_lon):
            flat[pl.ds(p * cap, cap), :] = sea_recv[p, f]
        arrived_out[f] = lax.dot_general(
            at_slot, flat[...], (((0,), (0,)), ((), ())),
            precision=lax.Precision.HIGHEST, preferred_element_type=jnp.float32,
        )[:n_block]

    for d in near:
        ice_copy[d].wait_recv()
    for f in range(2):
        for p in range(n_lon):
            flat[pl.ds(p * cap, cap), :] = ice_recv[p, f]
        blocks[f] = exact_dot(from_slots, flat[...])
        for i in range(rows):
            for c in range(cols // BX):
                ext[7 + f, pl.ds(top + i, 1), pl.ds(c * BX, BX)] = blocks[
                    f, pl.ds((i // BY) * (cols // BX) + c, 1), pl.ds((i % BY) * BX, BX)
                ]
    row_finish(row_start(1, 7, 2))
    col_finish(1, 7, 2, col_start(1, 7, 2))
    for d in near:
        pos_copy[d].wait_send()
        sea_copy[d].wait_send()
        ice_copy[d].wait_send()

    inv[...] = 1.0 / (2.0 * ext[7, span, :] + 1.0)

    @pl.when(jnp.logical_not(not_south))
    def _():
        inv[pl.ds(0, HALO), :] = jnp.zeros((HALO, wide), jnp.float32)

    def across(x):
        return pltpu.roll(x, wide - 1, 1) - pltpu.roll(x, 1, 1)

    sub = lax.broadcasted_iota(jnp.int32, (8, wide), 0)
    is_first = sub == 0
    is_last = sub == 7

    def three(f, r):
        return (
            ext[f, pl.ds(pl.multiple_of(r - 8, 8), 8), :],
            ext[f, pl.ds(r, 8), :],
            ext[f, pl.ds(pl.multiple_of(r + 8, 8), 8), :],
        )

    def upward(strips):
        below, here, above = strips
        return pltpu.roll(jnp.where(is_first, above, here), 7, 0) - pltpu.roll(
            jnp.where(is_last, below, here), 1, 0
        )

    scale = 1.0 / (1.0 + RELAX)

    def stress_strip(i, carry):
        r = pl.multiple_of(PAD + i * 8, 8)
        at = pl.ds(r, 8)
        u = three(0, r)
        v = three(1, r)
        u_y, v_y, u_x, v_x = upward(u), upward(v), across(u[1]), across(v[1])
        divu = (u_x + v_y) * 0.5
        tension = (u_x - v_y) * 0.5
        shear = (u_y + v_x) * 0.5
        square = divu * divu + (tension * tension + shear * shear) * 0.25 + 0.01
        strength = ext[8, at, :]
        ratio = strength * lax.rsqrt(square)
        ext[2, at, :] = (ext[2, at, :] + RELAX * (ratio * divu - strength)) * scale
        ratio = ratio * scale
        ext[3, at, :] = ext[3, at, :] * scale + (RELAX / 4.0) * (ratio * tension)
        ext[4, at, :] = ext[4, at, :] * scale + (RELAX / 8.0) * (ratio * shear)
        return carry

    def speed_strip(i, carry):
        r = pl.multiple_of(PAD + i * 8, 8)
        at = pl.ds(r, 8)
        one = three(2, r)
        two = three(3, r)
        mixed = three(4, r)
        s_x = across(one[1] + two[1])
        s_y = upward([x - y for x, y in zip(one, two)])
        c_x = across(mixed[1])
        c_y = upward(mixed)
        force_x = s_x * 0.25 + c_y * 0.5
        force_y = c_x * 0.5 + s_y * 0.25
        mass = ext[7, at, :]
        factor = inv[pl.ds(pl.multiple_of(i * 8, 8), 8), :]
        u = ext[0, at, :]
        v = ext[1, at, :]
        turn = FCOR * mass
        inertia = 2.0 * mass
        ext[0, at, :] = (inertia * u + force_x + ext[5, at, :] + turn * v) * factor
        ext[1, at, :] = (inertia * v + force_y + ext[6, at, :] - turn * u) * factor
        return carry

    def step(k, carry):
        lax.fori_loop(0, tall // 8, stress_strip, 0)
        lax.fori_loop(0, tall // 8, speed_strip, 0)
        return carry

    lax.fori_loop(0, SUB, step, 0)

    for f in range(2):
        vel_out[f] = ext[f, body, main]
    for f in range(3):
        str_out[f] = ext[2 + f, body, main]


def shards(
    surface_temp, salinity, wind_stress, ocean_current, velocity, stress,
    ice_area, ice_volume, air_temp, ice_mask, curve_pos,
):
    n_grp = lax.axis_size("grp")
    n_lon = lax.axis_size("lon")
    rows, cols = surface_temp.shape
    n_block, n_cat, cells = ice_area.shape
    cap = 2 * n_block // n_lon
    n_slot = n_lon * cap
    wide = cols + LANES
    tall = rows + 2 * HALO
    pos = curve_pos.astype(jnp.float32)
    ocean = ice_mask > 0
    f32 = functools.partial(pltpu.VMEM, dtype=jnp.float32)
    vmem = pl.BlockSpec(memory_space=pltpu.VMEM)
    velocity_out, stress_out, arrived = pl.pallas_call(
        functools.partial(coupled_kernel, n_grp, n_lon),
        out_shape=(
            jax.ShapeDtypeStruct(velocity.shape, jnp.float32),
            jax.ShapeDtypeStruct(stress.shape, jnp.float32),
            jax.ShapeDtypeStruct((2, n_block, cells), jnp.float32),
        ),
        in_specs=[vmem] * 12,
        out_specs=(vmem, vmem, vmem),
        scratch_shapes=[
            f32((N_FIELD, tall + 2 * PAD, wide)),
            f32((tall, wide)),
            f32((N_FIELD, HALO, cols)),
            f32((2, tall, LANES)),
            f32((2, tall, LANES)),
            f32((2, tall, LANES)),
            f32((2, tall, LANES)),
            f32((2, n_block, cells)),
            f32((n_slot, cells)),
            f32((3, n_block, cells)),
            f32((n_lon, 3, cap, cells)),
            f32((n_lon, cap, LANES)),
            f32((n_lon, cap, LANES)),
            f32((n_lon, 2, cap, cells)),
            f32((n_lon, 2, cap, cells)),
            f32((n_lon, 2, cap, cells)),
            f32((n_lon, 2, cap, cells)),
            pltpu.SemaphoreType.DMA((2, 2)),
            pltpu.SemaphoreType.DMA((2, 2)),
            pltpu.SemaphoreType.DMA((2, 2)),
            pltpu.SemaphoreType.DMA((2, 2)),
            pltpu.SemaphoreType.DMA((3, n_lon)),
            pltpu.SemaphoreType.DMA((3, n_lon)),
        ],
        compiler_params=pltpu.CompilerParams(
            collective_id=1, has_side_effects=True, vmem_limit_bytes=48 << 20
        ),
        name="coupled",
    )(
        pos[None, :], pos[:, None], ocean.astype(jnp.float32)[:, None],
        surface_temp, salinity, wind_stress, ocean_current, velocity, stress,
        ice_area.transpose(1, 0, 2), ice_volume.transpose(1, 0, 2), air_temp,
    )
    area_out, volume_out = thermo(
        ice_area, ice_volume, air_temp, arrived[0], arrived[1], ocean
    )
    return (velocity_out, stress_out, area_out, volume_out)


def solution(mesh):
    return jax.shard_map(
        shards,
        mesh=mesh,
        in_specs=(
            P("grp", "lon"),
            P("grp", "lon"),
            P(None, "grp", "lon"),
            P(None, "grp", "lon"),
            P(None, "grp", "lon"),
            P(None, "grp", "lon"),
            P(("grp", "lon"), None, None),
            P(("grp", "lon"), None, None),
            P(("grp", "lon"), None),
            P(("grp", "lon")),
            P(("grp", "lon")),
        ),
        out_specs=(
            P(None, "grp", "lon"),
            P(None, "grp", "lon"),
            P(("grp", "lon"), None, None),
            P(("grp", "lon"), None, None),
        ),
        check_vma=False,
    )
```

```python
import functools

import jax
import jax.numpy as jnp
from jax import lax
from jax.experimental import pallas as pl
from jax.experimental.pallas import tpu as pltpu
from jax.sharding import PartitionSpec as P

BY = 8
BX = 256
SUB = 4

KAPPA = 0.02
MELT = 0.6
PSTAR = 10.0
CSTAR = 20.0
RELAX = 0.4
FCOR = 0.3

HALO = 2 * SUB
PAD = 8
LANES = 128
MESH = pl.DeviceIdType.MESH

N_FIELD = 9


def thermo(area, volume, air, temp_blocks, salt_blocks, ocean):
    freeze = -0.054 * salt_blocks
    excess = temp_blocks - freeze
    growth = KAPPA * area * (freeze - air)[:, None, :] / (volume + 0.1)
    vol_new = (volume + growth) * jnp.exp(-MELT * excess)[:, None, :]
    area_new = area * jnp.exp(-0.5 * MELT * excess)[:, None, :]
    keep = ocean[:, None, None]
    area_keep = jnp.where(keep, area_new, area)
    volume_keep = jnp.where(keep, vol_new, volume)
    return (area_keep, volume_keep)


def exact_dot(a, b):
    return jnp.dot(a, b, precision=lax.Precision.HIGHEST, preferred_element_type=jnp.float32)


def coupled_kernel(
    n_grp, n_lon, pos_ref, mask_ref, temp_hbm, salt_hbm, wind_hbm, cur_hbm,
    vel_hbm, str_hbm, area_hbm, volume_hbm, air_hbm, vel_out, str_out, arrived_out,
    temp_ref, salt_ref, wind_ref, cur_ref, area_ref, volume_ref, air_ref, load_sem, ext, inv, mir, out_e, out_w, in_w, in_e,
    blocks, flat, sums, slot_sums, pos_send, pos_recv, sea_send, sea_recv, ice_send, ice_recv,
    row_send, row_recv, col_send, col_recv, a2a_send, a2a_recv,
):
    rows, cols = temp_ref.shape
    wide = cols + LANES
    top = PAD + HALO
    tall = rows + 2 * HALO
    n_block, cells = air_ref.shape
    cap = sea_send.shape[2]
    n_slot = n_lon * cap
    g = lax.axis_index("grp")
    l = lax.axis_index("lon")
    east = lax.rem(l + 1, n_lon)
    west = lax.rem(l + n_lon - 1, n_lon)
    mirror = n_lon - 1 - l
    not_south = g > 0
    not_north = g < n_grp - 1

    barrier = pltpu.get_barrier_semaphore()

    def peer(d):
        return lax.rem(l + d, n_lon)

    def source(d):
        return lax.rem(l + n_lon - d, n_lon)

    for d in range(1, n_lon):
        pl.semaphore_signal(
            barrier, inc=1, device_id={"grp": g, "lon": peer(d)}, device_id_type=MESH
        )

    @pl.when(not_south)
    def _():
        pl.semaphore_signal(
            barrier, inc=1, device_id={"grp": g - 1, "lon": l}, device_id_type=MESH
        )

    @pl.when(not_north)
    def _():
        pl.semaphore_signal(
            barrier, inc=1, device_id={"grp": g + 1, "lon": l}, device_id_type=MESH
        )

    body = pl.ds(top, rows)
    main = pl.ds(0, cols)
    loads = [
        pltpu.make_async_copy(src, dst, load_sem.at[k])
        for k, (src, dst) in enumerate(
            (
                (temp_hbm, temp_ref),
                (salt_hbm, salt_ref),
                (vel_hbm, ext.at[pl.ds(0, 2), body, main]),
                (str_hbm, ext.at[pl.ds(2, 3), body, main]),
                (wind_hbm, wind_ref),
                (cur_hbm, cur_ref),
                (area_hbm, area_ref),
                (volume_hbm, volume_ref),
                (air_hbm, air_ref),
            )
        )
    ]
    for load in loads:
        load.start()

    near = sorted(range(1, n_lon), key=lambda d: (min(d, n_lon - d), d))
    far = near[::-1]

    pos_row = pos_ref[...].astype(jnp.float32)
    down = lax.broadcasted_iota(jnp.int32, (n_block, n_block), 0)
    along = lax.broadcasted_iota(jnp.int32, (n_block, n_block), 1)

    def column(row):
        return jnp.sum(jnp.where(down == along, row, 0.0), axis=1, keepdims=True)

    keep = column(mask_ref[...].astype(jnp.float32)) > 0.0
    to_row = jnp.floor(pos_row * (1.0 / n_block))
    to_col = column(to_row)
    same = to_col == to_row
    rank_row = jnp.sum(jnp.where(same & (down < along), 1.0, 0.0), axis=0, keepdims=True)
    rank_col = jnp.sum(jnp.where(same & (along < down), 1.0, 0.0), axis=1, keepdims=True)
    slot_row = to_row * cap + rank_row
    slot_col = to_col * cap + rank_col
    slot_down = lax.broadcasted_iota(jnp.int32, (n_slot, n_block), 0).astype(jnp.float32)
    slot_along = lax.broadcasted_iota(jnp.int32, (n_block, n_slot), 1).astype(jnp.float32)
    to_slots = jnp.where(slot_down == slot_row, 1.0, 0.0)
    from_slots = jnp.where(slot_along == slot_col, 1.0, 0.0)
    pos_slot = jnp.sum(to_slots * (pos_row + 1.0), axis=1, keepdims=True) - 1.0
    pos_wide = jnp.broadcast_to(pos_slot, (n_slot, LANES))
    for p in range(n_lon):
        pos_send[p] = pos_wide[p * cap : (p + 1) * cap]

    loads[0].wait()
    loads[1].wait()
    for f, ref in enumerate((temp_ref, salt_ref)):
        for i in range(rows):
            for c in range(cols // BX):
                blocks[f, pl.ds((i // BY) * (cols // BX) + c, 1), pl.ds((i % BY) * BX, BX)] = ref[
                    pl.ds(i, 1), pl.ds(c * BX, BX)
                ]
    for f in range(2):
        packed = exact_dot(to_slots, blocks[f])
        for p in range(n_lon):
            sea_send[p, f] = packed[p * cap : (p + 1) * cap]

    pl.semaphore_wait(
        barrier, n_lon - 1 + jnp.where(not_south, 1, 0) + jnp.where(not_north, 1, 0)
    )

    def lon_copy(kind, src, dst, d):
        return pltpu.make_async_remote_copy(
            src_ref=src.at[peer(d)], dst_ref=dst.at[l],
            send_sem=a2a_send.at[kind, d], recv_sem=a2a_recv.at[kind, d],
            device_id={"grp": g, "lon": peer(d)}, device_id_type=MESH,
        )

    pos_copy = {d: lon_copy(0, pos_send, pos_recv, d) for d in near}
    sea_copy = {d: lon_copy(1, sea_send, sea_recv, d) for d in near}
    ice_copy = {d: lon_copy(2, ice_send, ice_recv, d) for d in near}
    for d in far:
        pos_copy[d].start()
    for d in far:
        sea_copy[d].start()
    pos_recv[l] = pos_send[l]
    sea_recv[l] = sea_send[l]

    for load in loads[2:6]:
        load.wait()
    for f in range(2):
        ext[5 + f, body, main] = wind_ref[f] + cur_ref[f]
    for f in range(N_FIELD):
        ext[f, pl.ds(0, PAD), :] = jnp.zeros((PAD, wide), jnp.float32)
        ext[f, pl.ds(top + rows + HALO, PAD), :] = jnp.zeros((PAD, wide), jnp.float32)

    @pl.when(jnp.logical_not(not_south))
    def _():
        for f in range(N_FIELD):
            ext[f, pl.ds(PAD, HALO), main] = jnp.zeros((HALO, cols), jnp.float32)

    lane = lax.broadcasted_iota(jnp.int32, (tall, LANES), 1)
    span = pl.ds(PAD, tall)

    def row_start(part, lo, n):
        fs = pl.ds(lo, n)

        @pl.when(jnp.logical_not(not_north))
        def _():
            a = lax.broadcasted_iota(jnp.int32, (LANES, LANES), 0)
            b = lax.broadcasted_iota(jnp.int32, (LANES, LANES), 1)
            flip = (a + b == LANES - 1).astype(jnp.float32)
            count = cols // LANES
            edge = pl.ds(top + rows - HALO, HALO)
            x = jnp.concatenate(
                [
                    ext[fs, edge, pl.ds(c * LANES, LANES)].reshape(n * HALO, LANES)
                    for c in range(count)
                ],
                axis=0,
            )
            y = exact_dot(x, flip).reshape(count * n, HALO, LANES)
            row = lax.broadcasted_iota(jnp.int32, (count * n, HALO, LANES), 1)
            for step in (1, 2, 4):
                y = jnp.where(
                    row % (2 * step) < step,
                    pltpu.roll(y, HALO - step, 1),
                    pltpu.roll(y, step, 1),
                )
            for c in range(count):
                for k in range(n):
                    sign = -1.0 if lo + k in (0, 1, 5, 6) else 1.0
                    mir[lo + k, :, pl.ds(cols - (c + 1) * LANES, LANES)] = sign * y[c * n + k]

        low = ext.at[fs, pl.ds(PAD, HALO), main]
        high = ext.at[fs, pl.ds(top + rows, HALO), main]
        to_south = pltpu.make_async_remote_copy(
            src_ref=ext.at[fs, pl.ds(top, HALO), main], dst_ref=high,
            send_sem=row_send.at[part, 0], recv_sem=row_recv.at[part, 0],
            device_id={"grp": jnp.where(not_south, g - 1, g), "lon": l}, device_id_type=MESH,
        )
        to_north = pltpu.make_async_remote_copy(
            src_ref=ext.at[fs, pl.ds(top + rows - HALO, HALO), main], dst_ref=low,
            send_sem=row_send.at[part, 1], recv_sem=row_recv.at[part, 1],
            device_id={"grp": jnp.where(not_north, g + 1, g), "lon": l}, device_id_type=MESH,
        )
        to_mirror = pltpu.make_async_remote_copy(
            src_ref=mir.at[fs], dst_ref=high,
            send_sem=row_send.at[part, 1], recv_sem=row_recv.at[part, 0],
            device_id={"grp": g, "lon": mirror}, device_id_type=MESH,
        )

        @pl.when(not_south)
        def _():
            to_south.start()

        @pl.when(not_north)
        def _():
            to_north.start()

        @pl.when(jnp.logical_not(not_north))
        def _():
            to_mirror.start()

        return to_south, to_north, to_mirror

    def row_finish(copies):
        to_south, to_north, to_mirror = copies
        to_south.wait_recv()

        @pl.when(not_south)
        def _():
            to_north.wait_recv()

        @pl.when(not_south)
        def _():
            to_south.wait_send()

        @pl.when(not_north)
        def _():
            to_north.wait_send()

        @pl.when(jnp.logical_not(not_north))
        def _():
            to_mirror.wait_send()

    def col_start(part, lo, n):
        east_pack = jnp.zeros((tall, LANES), jnp.float32)
        west_pack = jnp.zeros((tall, LANES), jnp.float32)
        for k in range(n):
            here = (lane >= k * HALO) & (lane < (k + 1) * HALO)
            tail = ext[lo + k, span, pl.ds(cols - LANES, LANES)]
            head = ext[lo + k, span, pl.ds(0, LANES)]
            east_pack = jnp.where(here, pltpu.roll(tail, (k + 1) * HALO, 1), east_pack)
            west_pack = jnp.where(here, pltpu.roll(head, k * HALO, 1) if k else head, west_pack)
        out_e[part] = east_pack
        out_w[part] = west_pack
        to_east = pltpu.make_async_remote_copy(
            src_ref=out_e.at[part], dst_ref=in_w.at[part],
            send_sem=col_send.at[part, 0], recv_sem=col_recv.at[part, 0],
            device_id={"grp": g, "lon": east}, device_id_type=MESH,
        )
        to_west = pltpu.make_async_remote_copy(
            src_ref=out_w.at[part], dst_ref=in_e.at[part],
            send_sem=col_send.at[part, 1], recv_sem=col_recv.at[part, 1],
            device_id={"grp": g, "lon": west}, device_id_type=MESH,
        )
        to_east.start()
        to_west.start()
        return to_east, to_west

    def col_finish(part, lo, n, copies):
        for copy in copies:
            copy.wait()
        from_west = in_w[part]
        from_east = in_e[part]
        for k in range(n):
            e = pltpu.roll(from_east, LANES - k * HALO, 1) if k else from_east
            w = pltpu.roll(from_west, LANES - (k + 1) * HALO, 1)
            ext[lo + k, span, pl.ds(cols, LANES)] = jnp.where(
                lane < HALO, e, jnp.where(lane >= LANES - HALO, w, 0.0)
            )

    early_rows = row_start(0, 0, 7)

    for load in loads[6:]:
        load.wait()
    n_cat = area_ref.shape[0]
    chunk = 512

    def reduce_chunk(i, carry):
        at = pl.ds(pl.multiple_of(i * chunk, chunk), chunk)
        area_sum = jnp.zeros((n_block, chunk), jnp.float32)
        vol_sum = jnp.zeros((n_block, chunk), jnp.float32)
        rate = jnp.zeros((n_block, chunk), jnp.float32)
        for c in range(n_cat):
            area = area_ref[c, :, at]
            vol = volume_ref[c, :, at]
            area_sum = area_sum + area
            vol_sum = vol_sum + vol
            rate = rate + area / (vol + 0.1)
        rate = KAPPA * rate
        sums[0, :, at] = jnp.where(keep, area_sum, 0.0)
        sums[1, :, at] = jnp.where(keep, vol_sum - rate * air_ref[:, at], 0.0)
        sums[2, :, at] = jnp.where(keep, rate, 0.0)
        return carry

    lax.fori_loop(0, cells // chunk, reduce_chunk, 0)

    for d in near:
        pos_copy[d].wait_recv()
    base = (l * n_block).astype(jnp.float32)
    for p in range(n_lon):
        flat[pl.ds(p * cap, cap), pl.ds(0, LANES)] = pos_recv[p]
    local = flat[:, pl.ds(0, LANES)] - base
    block_along = lax.broadcasted_iota(jnp.int32, (n_slot, LANES), 1).astype(jnp.float32)
    at_slot = jnp.where((local == block_along) & (block_along < n_block), 1.0, 0.0)
    for f in range(3):
        gathered = exact_dot(at_slot[:, :n_block], sums[f])
        for p in range(n_lon):
            slot_sums[p, f] = gathered[p * cap : (p + 1) * cap]

    row_finish(early_rows)
    early_cols = col_start(0, 0, 7)

    def answer(p):
        freeze = -0.054 * sea_recv[p, 1]
        decay = jnp.exp((-0.5 * MELT) * (sea_recv[p, 0] - freeze))
        mass = (slot_sums[p, 1] + slot_sums[p, 2] * freeze) * (decay * decay)
        conc = slot_sums[p, 0] * decay
        return mass, PSTAR * mass * jnp.exp(-CSTAR * (1.0 - conc))

    own_mass, own_strength = answer(l)
    ice_recv[l, 0] = own_mass
    ice_recv[l, 1] = own_strength
    for d in near:
        sea_copy[d].wait_recv()
        mass, strength = answer(source(d))
        ice_send[source(d), 0] = mass
        ice_send[source(d), 1] = strength
        ice_copy[n_lon - d].start()

    col_finish(0, 0, 7, early_cols)

    for f in range(2):
        for p in range(n_lon):
            flat[pl.ds(p * cap, cap), :] = sea_recv[p, f]
        arrived_out[f] = lax.dot_general(
            at_slot, flat[...], (((0,), (0,)), ((), ())),
            precision=lax.Precision.HIGHEST, preferred_element_type=jnp.float32,
        )[:n_block]

    for d in near:
        ice_copy[d].wait_recv()
    for f in range(2):
        for p in range(n_lon):
            flat[pl.ds(p * cap, cap), :] = ice_recv[p, f]
        blocks[f] = exact_dot(from_slots, flat[...])
        for i in range(rows):
            for c in range(cols // BX):
                ext[7 + f, pl.ds(top + i, 1), pl.ds(c * BX, BX)] = blocks[
                    f, pl.ds((i // BY) * (cols // BX) + c, 1), pl.ds((i % BY) * BX, BX)
                ]
    row_finish(row_start(1, 7, 2))
    col_finish(1, 7, 2, col_start(1, 7, 2))
    for d in near:
        pos_copy[d].wait_send()
        sea_copy[d].wait_send()
        ice_copy[d].wait_send()

    inv[...] = 1.0 / (2.0 * ext[7, span, :] + 1.0)

    @pl.when(jnp.logical_not(not_south))
    def _():
        inv[pl.ds(0, HALO), :] = jnp.zeros((HALO, wide), jnp.float32)

    def across(x):
        return pltpu.roll(x, wide - 1, 1) - pltpu.roll(x, 1, 1)

    sub = lax.broadcasted_iota(jnp.int32, (8, wide), 0)
    is_first = sub == 0
    is_last = sub == 7

    def three(f, r):
        return (
            ext[f, pl.ds(pl.multiple_of(r - 8, 8), 8), :],
            ext[f, pl.ds(r, 8), :],
            ext[f, pl.ds(pl.multiple_of(r + 8, 8), 8), :],
        )

    def upward(strips):
        below, here, above = strips
        return pltpu.roll(jnp.where(is_first, above, here), 7, 0) - pltpu.roll(
            jnp.where(is_last, below, here), 1, 0
        )

    scale = 1.0 / (1.0 + RELAX)

    def stress_strip(i, carry):
        r = pl.multiple_of(PAD + i * 8, 8)
        at = pl.ds(r, 8)
        u = three(0, r)
        v = three(1, r)
        u_y, v_y, u_x, v_x = upward(u), upward(v), across(u[1]), across(v[1])
        divu = (u_x + v_y) * 0.5
        tension = (u_x - v_y) * 0.5
        shear = (u_y + v_x) * 0.5
        square = divu * divu + (tension * tension + shear * shear) * 0.25 + 0.01
        strength = ext[8, at, :]
        ratio = strength * lax.rsqrt(square)
        ext[2, at, :] = (ext[2, at, :] + RELAX * (ratio * divu - strength)) * scale
        ratio = ratio * scale
        ext[3, at, :] = ext[3, at, :] * scale + (RELAX / 4.0) * (ratio * tension)
        ext[4, at, :] = ext[4, at, :] * scale + (RELAX / 8.0) * (ratio * shear)
        return carry

    def speed_strip(i, carry):
        r = pl.multiple_of(PAD + i * 8, 8)
        at = pl.ds(r, 8)
        one = three(2, r)
        two = three(3, r)
        mixed = three(4, r)
        s_x = across(one[1] + two[1])
        s_y = upward([x - y for x, y in zip(one, two)])
        c_x = across(mixed[1])
        c_y = upward(mixed)
        force_x = s_x * 0.25 + c_y * 0.5
        force_y = c_x * 0.5 + s_y * 0.25
        mass = ext[7, at, :]
        factor = inv[pl.ds(pl.multiple_of(i * 8, 8), 8), :]
        u = ext[0, at, :]
        v = ext[1, at, :]
        turn = FCOR * mass
        inertia = 2.0 * mass
        ext[0, at, :] = (inertia * u + force_x + ext[5, at, :] + turn * v) * factor
        ext[1, at, :] = (inertia * v + force_y + ext[6, at, :] - turn * u) * factor
        return carry

    def step(k, carry):
        lax.fori_loop(0, tall // 8, stress_strip, 0)
        lax.fori_loop(0, tall // 8, speed_strip, 0)
        return carry

    lax.fori_loop(0, SUB, step, 0)

    for f in range(2):
        vel_out[f] = ext[f, body, main]
    for f in range(3):
        str_out[f] = ext[2 + f, body, main]


def shards(
    surface_temp, salinity, wind_stress, ocean_current, velocity, stress,
    ice_area, ice_volume, air_temp, ice_mask, curve_pos,
):
    n_grp = lax.axis_size("grp")
    n_lon = lax.axis_size("lon")
    rows, cols = surface_temp.shape
    n_block, n_cat, cells = ice_area.shape
    cap = 2 * n_block // n_lon
    n_slot = n_lon * cap
    wide = cols + LANES
    tall = rows + 2 * HALO
    ocean = ice_mask > 0
    f32 = functools.partial(pltpu.VMEM, dtype=jnp.float32)
    vmem = pl.BlockSpec(memory_space=pltpu.VMEM)
    velocity_out, stress_out, arrived = pl.pallas_call(
        functools.partial(coupled_kernel, n_grp, n_lon),
        out_shape=(
            jax.ShapeDtypeStruct(velocity.shape, jnp.float32),
            jax.ShapeDtypeStruct(stress.shape, jnp.float32),
            jax.ShapeDtypeStruct((2, n_block, cells), jnp.float32),
        ),
        in_specs=[vmem] * 2 + [pl.BlockSpec(memory_space=pltpu.HBM)] * 9,
        out_specs=(vmem, vmem, vmem),
        scratch_shapes=[
            f32((rows, cols)),
            f32((rows, cols)),
            f32((2, rows, cols)),
            f32((2, rows, cols)),
            f32((n_cat, n_block, cells)),
            f32((n_cat, n_block, cells)),
            f32((n_block, cells)),
            pltpu.SemaphoreType.DMA((9,)),
            f32((N_FIELD, tall + 2 * PAD, wide)),
            f32((tall, wide)),
            f32((N_FIELD, HALO, cols)),
            f32((2, tall, LANES)),
            f32((2, tall, LANES)),
            f32((2, tall, LANES)),
            f32((2, tall, LANES)),
            f32((2, n_block, cells)),
            f32((n_slot, cells)),
            f32((3, n_block, cells)),
            f32((n_lon, 3, cap, cells)),
            f32((n_lon, cap, LANES)),
            f32((n_lon, cap, LANES)),
            f32((n_lon, 2, cap, cells)),
            f32((n_lon, 2, cap, cells)),
            f32((n_lon, 2, cap, cells)),
            f32((n_lon, 2, cap, cells)),
            pltpu.SemaphoreType.DMA((2, 2)),
            pltpu.SemaphoreType.DMA((2, 2)),
            pltpu.SemaphoreType.DMA((2, 2)),
            pltpu.SemaphoreType.DMA((2, 2)),
            pltpu.SemaphoreType.DMA((3, n_lon)),
            pltpu.SemaphoreType.DMA((3, n_lon)),
        ],
        compiler_params=pltpu.CompilerParams(
            collective_id=1, has_side_effects=True, vmem_limit_bytes=62 << 20
        ),
        name="coupled",
    )(
        curve_pos[None, :], ice_mask[None, :],
        surface_temp, salinity, wind_stress, ocean_current, velocity, stress,
        ice_area.transpose(1, 0, 2), ice_volume.transpose(1, 0, 2), air_temp,
    )
    area_out, volume_out = thermo(
        ice_area, ice_volume, air_temp, arrived[0], arrived[1], ocean
    )
    return (velocity_out, stress_out, area_out, volume_out)


def solution(mesh):
    return jax.shard_map(
        shards,
        mesh=mesh,
        in_specs=(
            P("grp", "lon"),
            P("grp", "lon"),
            P(None, "grp", "lon"),
            P(None, "grp", "lon"),
            P(None, "grp", "lon"),
            P(None, "grp", "lon"),
            P(("grp", "lon"), None, None),
            P(("grp", "lon"), None, None),
            P(("grp", "lon"), None),
            P(("grp", "lon")),
            P(("grp", "lon")),
        ),
        out_specs=(
            P(None, "grp", "lon"),
            P(None, "grp", "lon"),
            P(("grp", "lon"), None, None),
            P(("grp", "lon"), None, None),
        ),
        check_vma=False,
    )
```

```python
import functools

import jax
import jax.numpy as jnp
from jax import lax
from jax.experimental import pallas as pl
from jax.experimental.pallas import tpu as pltpu
from jax.sharding import PartitionSpec as P

BY = 8
BX = 256
SUB = 4

KAPPA = 0.02
MELT = 0.6
PSTAR = 10.0
CSTAR = 20.0
RELAX = 0.4
FCOR = 0.3

HALO = 2 * SUB
PAD = 8
LANES = 128
MESH = pl.DeviceIdType.MESH

N_FIELD = 9


def thermo(area, volume, air, temp_blocks, salt_blocks, ocean):
    freeze = -0.054 * salt_blocks
    excess = temp_blocks - freeze
    growth = KAPPA * area * (freeze - air)[:, None, :] / (volume + 0.1)
    vol_new = (volume + growth) * jnp.exp(-MELT * excess)[:, None, :]
    area_new = area * jnp.exp(-0.5 * MELT * excess)[:, None, :]
    keep = ocean[:, None, None]
    area_keep = jnp.where(keep, area_new, area)
    volume_keep = jnp.where(keep, vol_new, volume)
    return (area_keep, volume_keep)


def exact_dot(a, b):
    return jnp.dot(a, b, precision=lax.Precision.HIGHEST, preferred_element_type=jnp.float32)


def coupled_kernel(
    n_grp, n_lon, pos_ref, mask_ref, temp_hbm, salt_hbm, wind_hbm, cur_hbm,
    vel_hbm, str_hbm, area_hbm, volume_hbm, air_hbm, vel_out, str_out, arrived_out,
    temp_ref, salt_ref, wind_ref, cur_ref, area_ref, volume_ref, air_ref, load_sem, ext, inv, mir, out_e, out_w, in_w, in_e,
    blocks, flat, sums, slot_sums, pos_send, pos_recv, sea_send, sea_recv, ice_send, ice_recv,
    row_send, row_recv, col_send, col_recv, a2a_send, a2a_recv,
):
    rows, cols = temp_ref.shape
    wide = cols + LANES
    top = PAD + HALO
    tall = rows + 2 * HALO
    n_block, cells = air_ref.shape
    cap = sea_send.shape[2]
    n_slot = n_lon * cap
    g = lax.axis_index("grp")
    l = lax.axis_index("lon")
    east = lax.rem(l + 1, n_lon)
    west = lax.rem(l + n_lon - 1, n_lon)
    mirror = n_lon - 1 - l
    not_south = g > 0
    not_north = g < n_grp - 1

    barrier = pltpu.get_barrier_semaphore()

    def peer(d):
        return lax.rem(l + d, n_lon)

    def source(d):
        return lax.rem(l + n_lon - d, n_lon)

    for d in range(1, n_lon):
        pl.semaphore_signal(
            barrier, inc=1, device_id={"grp": g, "lon": peer(d)}, device_id_type=MESH
        )

    @pl.when(not_south)
    def _():
        pl.semaphore_signal(
            barrier, inc=1, device_id={"grp": g - 1, "lon": l}, device_id_type=MESH
        )

    @pl.when(not_north)
    def _():
        pl.semaphore_signal(
            barrier, inc=1, device_id={"grp": g + 1, "lon": l}, device_id_type=MESH
        )

    body = pl.ds(top, rows)
    main = pl.ds(0, cols)
    loads = [
        pltpu.make_async_copy(src, dst, load_sem.at[k])
        for k, (src, dst) in enumerate(
            (
                (temp_hbm, temp_ref),
                (salt_hbm, salt_ref),
                (vel_hbm, ext.at[pl.ds(0, 2), body, main]),
                (str_hbm, ext.at[pl.ds(2, 3), body, main]),
                (wind_hbm, wind_ref),
                (cur_hbm, cur_ref),
                (area_hbm, area_ref),
                (volume_hbm, volume_ref),
                (air_hbm, air_ref),
            )
        )
    ]
    for load in loads:
        load.start()

    near = sorted(range(1, n_lon), key=lambda d: (min(d, n_lon - d), d))
    far = near[::-1]

    for load in loads[2:6]:
        load.wait()
    for f in range(2):
        ext[5 + f, body, main] = wind_ref[f] + cur_ref[f]
    for f in range(N_FIELD):
        ext[f, pl.ds(0, PAD), :] = jnp.zeros((PAD, wide), jnp.float32)
        ext[f, pl.ds(top + rows + HALO, PAD), :] = jnp.zeros((PAD, wide), jnp.float32)

    @pl.when(jnp.logical_not(not_south))
    def _():
        for f in range(N_FIELD):
            ext[f, pl.ds(PAD, HALO), main] = jnp.zeros((HALO, cols), jnp.float32)

    lane = lax.broadcasted_iota(jnp.int32, (tall, LANES), 1)
    span = pl.ds(PAD, tall)

    def row_start(part, lo, n):
        fs = pl.ds(lo, n)

        low = ext.at[fs, pl.ds(PAD, HALO), main]
        high = ext.at[fs, pl.ds(top + rows, HALO), main]
        to_south = pltpu.make_async_remote_copy(
            src_ref=ext.at[fs, pl.ds(top, HALO), main], dst_ref=high,
            send_sem=row_send.at[part, 0], recv_sem=row_recv.at[part, 0],
            device_id={"grp": jnp.where(not_south, g - 1, g), "lon": l}, device_id_type=MESH,
        )
        to_north = pltpu.make_async_remote_copy(
            src_ref=ext.at[fs, pl.ds(top + rows - HALO, HALO), main], dst_ref=low,
            send_sem=row_send.at[part, 1], recv_sem=row_recv.at[part, 1],
            device_id={"grp": jnp.where(not_north, g + 1, g), "lon": l}, device_id_type=MESH,
        )
        to_mirror = pltpu.make_async_remote_copy(
            src_ref=mir.at[fs], dst_ref=high,
            send_sem=row_send.at[part, 1], recv_sem=row_recv.at[part, 0],
            device_id={"grp": g, "lon": mirror}, device_id_type=MESH,
        )

        @pl.when(not_south)
        def _():
            to_south.start()

        @pl.when(not_north)
        def _():
            to_north.start()

        @pl.when(jnp.logical_not(not_north))
        def _():
            a = lax.broadcasted_iota(jnp.int32, (LANES, LANES), 0)
            b = lax.broadcasted_iota(jnp.int32, (LANES, LANES), 1)
            flip = (a + b == LANES - 1).astype(jnp.float32)
            count = cols // LANES
            edge = pl.ds(top + rows - HALO, HALO)
            x = jnp.concatenate(
                [
                    ext[fs, edge, pl.ds(c * LANES, LANES)].reshape(n * HALO, LANES)
                    for c in range(count)
                ],
                axis=0,
            )
            y = exact_dot(x, flip).reshape(count * n, HALO, LANES)
            row = lax.broadcasted_iota(jnp.int32, (count * n, HALO, LANES), 1)
            for step in (1, 2, 4):
                y = jnp.where(
                    row % (2 * step) < step,
                    pltpu.roll(y, HALO - step, 1),
                    pltpu.roll(y, step, 1),
                )
            for c in range(count):
                for k in range(n):
                    sign = -1.0 if lo + k in (0, 1, 5, 6) else 1.0
                    mir[lo + k, :, pl.ds(cols - (c + 1) * LANES, LANES)] = sign * y[c * n + k]
            to_mirror.start()

        return to_south, to_north, to_mirror

    def row_finish(copies):
        to_south, to_north, to_mirror = copies
        to_south.wait_recv()

        @pl.when(not_south)
        def _():
            to_north.wait_recv()

        @pl.when(not_south)
        def _():
            to_south.wait_send()

        @pl.when(not_north)
        def _():
            to_north.wait_send()

        @pl.when(jnp.logical_not(not_north))
        def _():
            to_mirror.wait_send()

    def col_start(part, lo, n):
        east_pack = jnp.zeros((tall, LANES), jnp.float32)
        west_pack = jnp.zeros((tall, LANES), jnp.float32)
        for k in range(n):
            here = (lane >= k * HALO) & (lane < (k + 1) * HALO)
            tail = ext[lo + k, span, pl.ds(cols - LANES, LANES)]
            head = ext[lo + k, span, pl.ds(0, LANES)]
            east_pack = jnp.where(here, pltpu.roll(tail, (k + 1) * HALO, 1), east_pack)
            west_pack = jnp.where(here, pltpu.roll(head, k * HALO, 1) if k else head, west_pack)
        out_e[part] = east_pack
        out_w[part] = west_pack
        to_east = pltpu.make_async_remote_copy(
            src_ref=out_e.at[part], dst_ref=in_w.at[part],
            send_sem=col_send.at[part, 0], recv_sem=col_recv.at[part, 0],
            device_id={"grp": g, "lon": east}, device_id_type=MESH,
        )
        to_west = pltpu.make_async_remote_copy(
            src_ref=out_w.at[part], dst_ref=in_e.at[part],
            send_sem=col_send.at[part, 1], recv_sem=col_recv.at[part, 1],
            device_id={"grp": g, "lon": west}, device_id_type=MESH,
        )
        to_east.start()
        to_west.start()
        return to_east, to_west

    def col_finish(part, lo, n, copies):
        for copy in copies:
            copy.wait()
        from_west = in_w[part]
        from_east = in_e[part]
        for k in range(n):
            e = pltpu.roll(from_east, LANES - k * HALO, 1) if k else from_east
            w = pltpu.roll(from_west, LANES - (k + 1) * HALO, 1)
            ext[lo + k, span, pl.ds(cols, LANES)] = jnp.where(
                lane < HALO, e, jnp.where(lane >= LANES - HALO, w, 0.0)
            )

    pl.semaphore_wait(
        barrier, n_lon - 1 + jnp.where(not_south, 1, 0) + jnp.where(not_north, 1, 0)
    )

    early_rows = row_start(0, 0, 7)

    pos_row = pos_ref[...].astype(jnp.float32)
    down = lax.broadcasted_iota(jnp.int32, (n_block, n_block), 0)
    along = lax.broadcasted_iota(jnp.int32, (n_block, n_block), 1)

    def column(row):
        return jnp.sum(jnp.where(down == along, row, 0.0), axis=1, keepdims=True)

    keep = column(mask_ref[...].astype(jnp.float32)) > 0.0
    to_row = jnp.floor(pos_row * (1.0 / n_block))
    to_col = column(to_row)
    same = to_col == to_row
    rank_row = jnp.sum(jnp.where(same & (down < along), 1.0, 0.0), axis=0, keepdims=True)
    rank_col = jnp.sum(jnp.where(same & (along < down), 1.0, 0.0), axis=1, keepdims=True)
    slot_row = to_row * cap + rank_row
    slot_col = to_col * cap + rank_col
    slot_down = lax.broadcasted_iota(jnp.int32, (n_slot, n_block), 0).astype(jnp.float32)
    slot_along = lax.broadcasted_iota(jnp.int32, (n_block, n_slot), 1).astype(jnp.float32)
    to_slots = jnp.where(slot_down == slot_row, 1.0, 0.0)
    from_slots = jnp.where(slot_along == slot_col, 1.0, 0.0)
    pos_slot = jnp.sum(to_slots * (pos_row + 1.0), axis=1, keepdims=True) - 1.0
    pos_wide = jnp.broadcast_to(pos_slot, (n_slot, LANES))
    for p in range(n_lon):
        pos_send[p] = pos_wide[p * cap : (p + 1) * cap]

    loads[0].wait()
    loads[1].wait()
    for f, ref in enumerate((temp_ref, salt_ref)):
        for i in range(rows):
            for c in range(cols // BX):
                blocks[f, pl.ds((i // BY) * (cols // BX) + c, 1), pl.ds((i % BY) * BX, BX)] = ref[
                    pl.ds(i, 1), pl.ds(c * BX, BX)
                ]
    for f in range(2):
        packed = exact_dot(to_slots, blocks[f])
        for p in range(n_lon):
            sea_send[p, f] = packed[p * cap : (p + 1) * cap]

    def lon_copy(kind, src, dst, d):
        return pltpu.make_async_remote_copy(
            src_ref=src.at[peer(d)], dst_ref=dst.at[l],
            send_sem=a2a_send.at[kind, d], recv_sem=a2a_recv.at[kind, d],
            device_id={"grp": g, "lon": peer(d)}, device_id_type=MESH,
        )

    pos_copy = {d: lon_copy(0, pos_send, pos_recv, d) for d in near}
    sea_copy = {d: lon_copy(1, sea_send, sea_recv, d) for d in near}
    ice_copy = {d: lon_copy(2, ice_send, ice_recv, d) for d in near}
    for d in far:
        pos_copy[d].start()
    for d in far:
        sea_copy[d].start()
    pos_recv[l] = pos_send[l]
    sea_recv[l] = sea_send[l]


    for load in loads[6:]:
        load.wait()
    n_cat = area_ref.shape[0]
    chunk = 512

    def reduce_chunk(i, carry):
        at = pl.ds(pl.multiple_of(i * chunk, chunk), chunk)
        area_sum = jnp.zeros((n_block, chunk), jnp.float32)
        vol_sum = jnp.zeros((n_block, chunk), jnp.float32)
        rate = jnp.zeros((n_block, chunk), jnp.float32)
        for c in range(n_cat):
            area = area_ref[c, :, at]
            vol = volume_ref[c, :, at]
            area_sum = area_sum + area
            vol_sum = vol_sum + vol
            rate = rate + area / (vol + 0.1)
        rate = KAPPA * rate
        sums[0, :, at] = jnp.where(keep, area_sum, 0.0)
        sums[1, :, at] = jnp.where(keep, vol_sum - rate * air_ref[:, at], 0.0)
        sums[2, :, at] = jnp.where(keep, rate, 0.0)
        return carry

    lax.fori_loop(0, cells // chunk, reduce_chunk, 0)

    for d in near:
        pos_copy[d].wait_recv()
    base = (l * n_block).astype(jnp.float32)
    for p in range(n_lon):
        flat[pl.ds(p * cap, cap), pl.ds(0, LANES)] = pos_recv[p]
    local = flat[:, pl.ds(0, LANES)] - base
    block_along = lax.broadcasted_iota(jnp.int32, (n_slot, LANES), 1).astype(jnp.float32)
    at_slot = jnp.where((local == block_along) & (block_along < n_block), 1.0, 0.0)
    for f in range(3):
        gathered = exact_dot(at_slot[:, :n_block], sums[f])
        for p in range(n_lon):
            slot_sums[p, f] = gathered[p * cap : (p + 1) * cap]

    row_finish(early_rows)
    early_cols = col_start(0, 0, 7)

    def answer(p):
        freeze = -0.054 * sea_recv[p, 1]
        decay = jnp.exp((-0.5 * MELT) * (sea_recv[p, 0] - freeze))
        mass = (slot_sums[p, 1] + slot_sums[p, 2] * freeze) * (decay * decay)
        conc = slot_sums[p, 0] * decay
        return mass, PSTAR * mass * jnp.exp(-CSTAR * (1.0 - conc))

    own_mass, own_strength = answer(l)
    ice_recv[l, 0] = own_mass
    ice_recv[l, 1] = own_strength
    for d in near:
        sea_copy[d].wait_recv()
        mass, strength = answer(source(d))
        ice_send[source(d), 0] = mass
        ice_send[source(d), 1] = strength
        ice_copy[n_lon - d].start()

    col_finish(0, 0, 7, early_cols)

    for f in range(2):
        for p in range(n_lon):
            flat[pl.ds(p * cap, cap), :] = sea_recv[p, f]
        arrived_out[f] = lax.dot_general(
            at_slot, flat[...], (((0,), (0,)), ((), ())),
            precision=lax.Precision.HIGHEST, preferred_element_type=jnp.float32,
        )[:n_block]

    for d in near:
        ice_copy[d].wait_recv()
    for f in range(2):
        for p in range(n_lon):
            flat[pl.ds(p * cap, cap), :] = ice_recv[p, f]
        blocks[f] = exact_dot(from_slots, flat[...])
        for i in range(rows):
            for c in range(cols // BX):
                ext[7 + f, pl.ds(top + i, 1), pl.ds(c * BX, BX)] = blocks[
                    f, pl.ds((i // BY) * (cols // BX) + c, 1), pl.ds((i % BY) * BX, BX)
                ]
    row_finish(row_start(1, 7, 2))
    col_finish(1, 7, 2, col_start(1, 7, 2))
    for d in near:
        pos_copy[d].wait_send()
        sea_copy[d].wait_send()
        ice_copy[d].wait_send()

    inv[...] = 1.0 / (2.0 * ext[7, span, :] + 1.0)

    @pl.when(jnp.logical_not(not_south))
    def _():
        inv[pl.ds(0, HALO), :] = jnp.zeros((HALO, wide), jnp.float32)

    def across(x):
        return pltpu.roll(x, wide - 1, 1) - pltpu.roll(x, 1, 1)

    sub = lax.broadcasted_iota(jnp.int32, (8, wide), 0)
    is_first = sub == 0
    is_last = sub == 7

    def three(f, r):
        return (
            ext[f, pl.ds(pl.multiple_of(r - 8, 8), 8), :],
            ext[f, pl.ds(r, 8), :],
            ext[f, pl.ds(pl.multiple_of(r + 8, 8), 8), :],
        )

    def upward(strips):
        below, here, above = strips
        return pltpu.roll(jnp.where(is_first, above, here), 7, 0) - pltpu.roll(
            jnp.where(is_last, below, here), 1, 0
        )

    scale = 1.0 / (1.0 + RELAX)

    def stress_strip(i, carry):
        r = pl.multiple_of(PAD + i * 8, 8)
        at = pl.ds(r, 8)
        u = three(0, r)
        v = three(1, r)
        u_y, v_y, u_x, v_x = upward(u), upward(v), across(u[1]), across(v[1])
        divu = (u_x + v_y) * 0.5
        tension = (u_x - v_y) * 0.5
        shear = (u_y + v_x) * 0.5
        square = divu * divu + (tension * tension + shear * shear) * 0.25 + 0.01
        strength = ext[8, at, :]
        ratio = strength * lax.rsqrt(square)
        ext[2, at, :] = (ext[2, at, :] + RELAX * (ratio * divu - strength)) * scale
        ratio = ratio * scale
        ext[3, at, :] = ext[3, at, :] * scale + (RELAX / 4.0) * (ratio * tension)
        ext[4, at, :] = ext[4, at, :] * scale + (RELAX / 8.0) * (ratio * shear)
        return carry

    def speed_strip(i, carry):
        r = pl.multiple_of(PAD + i * 8, 8)
        at = pl.ds(r, 8)
        one = three(2, r)
        two = three(3, r)
        mixed = three(4, r)
        s_x = across(one[1] + two[1])
        s_y = upward([x - y for x, y in zip(one, two)])
        c_x = across(mixed[1])
        c_y = upward(mixed)
        force_x = s_x * 0.25 + c_y * 0.5
        force_y = c_x * 0.5 + s_y * 0.25
        mass = ext[7, at, :]
        factor = inv[pl.ds(pl.multiple_of(i * 8, 8), 8), :]
        u = ext[0, at, :]
        v = ext[1, at, :]
        turn = FCOR * mass
        inertia = 2.0 * mass
        ext[0, at, :] = (inertia * u + force_x + ext[5, at, :] + turn * v) * factor
        ext[1, at, :] = (inertia * v + force_y + ext[6, at, :] - turn * u) * factor
        return carry

    def step(k, carry):
        lax.fori_loop(0, tall // 8, stress_strip, 0)
        lax.fori_loop(0, tall // 8, speed_strip, 0)
        return carry

    lax.fori_loop(0, SUB, step, 0)

    for f in range(2):
        vel_out[f] = ext[f, body, main]
    for f in range(3):
        str_out[f] = ext[2 + f, body, main]


def shards(
    surface_temp, salinity, wind_stress, ocean_current, velocity, stress,
    ice_area, ice_volume, air_temp, ice_mask, curve_pos,
):
    n_grp = lax.axis_size("grp")
    n_lon = lax.axis_size("lon")
    rows, cols = surface_temp.shape
    n_block, n_cat, cells = ice_area.shape
    cap = 2 * n_block // n_lon
    n_slot = n_lon * cap
    wide = cols + LANES
    tall = rows + 2 * HALO
    ocean = ice_mask > 0
    f32 = functools.partial(pltpu.VMEM, dtype=jnp.float32)
    vmem = pl.BlockSpec(memory_space=pltpu.VMEM)
    velocity_out, stress_out, arrived = pl.pallas_call(
        functools.partial(coupled_kernel, n_grp, n_lon),
        out_shape=(
            jax.ShapeDtypeStruct(velocity.shape, jnp.float32),
            jax.ShapeDtypeStruct(stress.shape, jnp.float32),
            jax.ShapeDtypeStruct((2, n_block, cells), jnp.float32),
        ),
        in_specs=[vmem] * 2 + [pl.BlockSpec(memory_space=pltpu.HBM)] * 9,
        out_specs=(vmem, vmem, vmem),
        scratch_shapes=[
            f32((rows, cols)),
            f32((rows, cols)),
            f32((2, rows, cols)),
            f32((2, rows, cols)),
            f32((n_cat, n_block, cells)),
            f32((n_cat, n_block, cells)),
            f32((n_block, cells)),
            pltpu.SemaphoreType.DMA((9,)),
            f32((N_FIELD, tall + 2 * PAD, wide)),
            f32((tall, wide)),
            f32((N_FIELD, HALO, cols)),
            f32((2, tall, LANES)),
            f32((2, tall, LANES)),
            f32((2, tall, LANES)),
            f32((2, tall, LANES)),
            f32((2, n_block, cells)),
            f32((n_slot, cells)),
            f32((3, n_block, cells)),
            f32((n_lon, 3, cap, cells)),
            f32((n_lon, cap, LANES)),
            f32((n_lon, cap, LANES)),
            f32((n_lon, 2, cap, cells)),
            f32((n_lon, 2, cap, cells)),
            f32((n_lon, 2, cap, cells)),
            f32((n_lon, 2, cap, cells)),
            pltpu.SemaphoreType.DMA((2, 2)),
            pltpu.SemaphoreType.DMA((2, 2)),
            pltpu.SemaphoreType.DMA((2, 2)),
            pltpu.SemaphoreType.DMA((2, 2)),
            pltpu.SemaphoreType.DMA((3, n_lon)),
            pltpu.SemaphoreType.DMA((3, n_lon)),
        ],
        compiler_params=pltpu.CompilerParams(
            collective_id=1, has_side_effects=True, vmem_limit_bytes=62 << 20
        ),
        name="coupled",
    )(
        curve_pos[None, :], ice_mask[None, :],
        surface_temp, salinity, wind_stress, ocean_current, velocity, stress,
        ice_area.transpose(1, 0, 2), ice_volume.transpose(1, 0, 2), air_temp,
    )
    area_out, volume_out = thermo(
        ice_area, ice_volume, air_temp, arrived[0], arrived[1], ocean
    )
    return (velocity_out, stress_out, area_out, volume_out)


def solution(mesh):
    return jax.shard_map(
        shards,
        mesh=mesh,
        in_specs=(
            P("grp", "lon"),
            P("grp", "lon"),
            P(None, "grp", "lon"),
            P(None, "grp", "lon"),
            P(None, "grp", "lon"),
            P(None, "grp", "lon"),
            P(("grp", "lon"), None, None),
            P(("grp", "lon"), None, None),
            P(("grp", "lon"), None),
            P(("grp", "lon")),
            P(("grp", "lon")),
        ),
        out_specs=(
            P(None, "grp", "lon"),
            P(None, "grp", "lon"),
            P(("grp", "lon"), None, None),
            P(("grp", "lon"), None, None),
        ),
        check_vma=False,
    )
```
